512 devices in a mesh: cells: 128 (over z, y_lo, x, core), stations: 4 (over y_hi).
Axes of the slice: x: 4, y: 8 (y_hi: 4, y_lo: 2; y = y_hi * 2 + y_lo), z: 8, core: 2. Of those that a mesh axis runs over, the one named last changes fastest.
Arguments:
- probes: bfloat16 [16, 524288], P(None, 'cells'), may hold values from -6 to 6
- reg_weight: float32 [524288], P('cells'), may hold values from 0.1 to 1
- cell_plan: int32 [2, 524288], P(None, 'cells'), may hold values from 0 to 255
- cell_depth: int32 [524288], P('cells'), may hold values from 0 to 15, as said below
- station_index: int32 [2, 16384], P(None, 'stations'), may hold values from 0 to 65535, as said below
- station_weight: float32 [16384], P('stations'), may hold values from 0.5 to 2
Outputs:
- basis: float32 [16, 524288], P(None, ('cells', 'stations'))
- factor: float32 [16, 16], replicated
The draws below stay inside these ranges and needn't reach their ends.
Inputs may be any that keep to these rules, and one draw needn't show every extreme that they name: `cell_plan`: east and north cell indices of a grid of 256 by 256 columns. `cell_depth`: depth indices of 16 layers. `station_index`: east and north station positions in 1/256ths of a cell width, over the same area as the cells' grid.
All inputs are finite; a program needn't handle non-finite values.
Results may differ from the reference program's by a relative error of at most 0.00065.
Values may be sent and summed in bfloat16 or wider, within the bound.
No kernel may reach another device: no remote copies, remote signals or barrier semaphores. Data moves between devices by JAX's collectives and lax.ppermute only.
A program may use at most 64 MiB of HBM per device.

```python
import math
import jax
import jax.numpy as jnp
from jax import lax

K = 16
CELLS = 524288
STATIONS = 16384


def draw_station_index(key, part):
    raw_points = jax.random.randint(key, (2, STATIONS), 0, 65536, dtype=jnp.int32)
    highest = jnp.max(raw_points, axis=1, keepdims=True)
    return raw_points + (65535 - highest)


def draw_cell_depth(key, part):
    positions = jnp.arange(CELLS, dtype=jnp.int32)
    layer_base = 15 - positions * 16 // CELLS
    jitter_steps = jax.random.randint(jax.random.fold_in(key, 7), (CELLS,), -2, 3, dtype=jnp.int32)
    return jnp.clip(layer_base + jitter_steps, 0, 15).astype(jnp.int32)


def set_ends(drawn, stream_key, smallest, largest):
    shape = drawn.shape
    place = [jax.random.randint(jax.random.fold_in(stream_key, axis), (), 0, shape[axis]) for axis in range(len(shape))]
    drawn = drawn.at[tuple(place)].set(smallest)
    longest = shape.index(max(shape))
    place[longest] = (place[longest] + 1) % shape[longest]
    return drawn.at[tuple(place)].set(largest)


def block_levels(rng, extent, cuts, low, high):
    factor_of, own = 1.0, jax.random.fold_in(rng, 6)
    for position, parts in cuts:
        steps = jnp.exp(jax.random.uniform(jax.random.fold_in(own, position), (parts,), jnp.float32, low / len(cuts), high / len(cuts)))
        factor_of = factor_of * jnp.repeat(steps, extent[position] // parts).reshape([-1 if axis == position else 1 for axis in range(len(extent))])
    return factor_of


def normal_values(key, extent, width, limit, cuts=(), kind=jnp.bfloat16):
    entries = width * jax.random.normal(key, extent, jnp.float32)
    if cuts:
        entries = entries * block_levels(key, extent, cuts, -0.22, 0.18)
    return jnp.clip(entries, -limit, limit).astype(kind)


def setup_inputs(seed: int = 0) -> dict:
    streams_of = jax.random.split(jax.random.key(seed), 7)
    probes = normal_values(streams_of[0], (K, CELLS), 1.0, 6.0, ((1, 128),))
    reg_weight = jnp.clip(jnp.exp(math.log(1.0) - 2.3025851 * jax.random.uniform(streams_of[1], (CELLS,), jnp.float32) ** block_levels(streams_of[1], (CELLS,), ((0, 128),), -0.2, 0.2)), 0.1, 1.0)
    cell_plan = set_ends(jax.random.randint(streams_of[2], (2, CELLS), 0, 256), jax.random.fold_in(streams_of[2], 1), 0, 255).astype(jnp.int32)
    cell_depth = draw_cell_depth(jax.random.fold_in(streams_of[6], 71), 0)
    station_index = draw_station_index(jax.random.fold_in(streams_of[6], 71), 0)
    station_weight = jnp.clip(jnp.exp(math.log(2.0) - 1.3862944 * jax.random.uniform(streams_of[5], (STATIONS,), jnp.float32) ** block_levels(streams_of[5], (STATIONS,), ((0, 4),), -0.2, 0.2)), 0.5, 2.0)
    return dict(probes=probes, reg_weight=reg_weight, cell_plan=cell_plan, cell_depth=cell_depth, station_index=station_index, station_weight=station_weight)


GRAVITY = 2.0
JITTER = 1e-06
SUBSTEP = 0.00390625

def cell_points(cell_plan, cell_depth):
    cell_east = cell_plan[0].astype(jnp.float32) + 0.5
    cell_north = cell_plan[1].astype(jnp.float32) + 0.5
    cell_down = cell_depth.astype(jnp.float32) + 1.0
    return (cell_east, cell_north, cell_down)

def sensitivity(st_east, st_north, cell_east, cell_north, cell_down):
    d_east = cell_east[None, :] - st_east[:, None]
    d_north = cell_north[None, :] - st_north[:, None]
    distance = d_east * d_east + d_north * d_north + cell_down[None, :] * cell_down[None, :]
    inverse = lax.rsqrt(distance)
    return (GRAVITY * cell_down[None, :] * inverse * inverse * inverse).astype(jnp.bfloat16)

def widened(sens_tile):
    return lax.optimization_barrier(sens_tile).astype(jnp.float32)

def reference(probes, reg_weight, cell_plan, cell_depth, station_index, station_weight):
    cell_east, cell_north, cell_down = cell_points(cell_plan, cell_depth)
    st_east = station_index[0].astype(jnp.float32) * SUBSTEP
    st_north = station_index[1].astype(jnp.float32) * SUBSTEP
    ref_block = math.gcd(STATIONS, 64)
    block_total = STATIONS // ref_block
    probe_wide = probes.astype(jnp.float32)

    def forward_block(turn_index):
        start_at = turn_index * ref_block
        sens_tile = widened(sensitivity(lax.dynamic_slice_in_dim(st_east, start_at, ref_block), lax.dynamic_slice_in_dim(st_north, start_at, ref_block), cell_east, cell_north, cell_down))
        return lax.dot_general(probe_wide.astype(jnp.float32), sens_tile.astype(jnp.float32), (((1,), (1,)), ((), ())), preferred_element_type=jnp.float32)
    stacked = lax.map(forward_block, jnp.arange(block_total, dtype=jnp.int32))
    station_field = jnp.transpose(stacked, (1, 0, 2)).reshape(K, STATIONS)
    weighted = (station_weight[None, :] * station_weight[None, :] * station_field).astype(jnp.bfloat16)
    weighted_wide = weighted.astype(jnp.float32)

    def backward_block(turn_index, running):
        start_at = turn_index * ref_block
        sens_tile = widened(sensitivity(lax.dynamic_slice_in_dim(st_east, start_at, ref_block), lax.dynamic_slice_in_dim(st_north, start_at, ref_block), cell_east, cell_north, cell_down))
        segment = lax.dynamic_slice_in_dim(weighted_wide, start_at, ref_block, 1)
        return running + jnp.dot(segment.astype(jnp.float32), sens_tile.astype(jnp.float32), preferred_element_type=jnp.float32)
    hess_image = lax.fori_loop(0, block_total, backward_block, jnp.zeros((K, CELLS), jnp.float32))
    hess_image = hess_image + reg_weight[None, :] * probe_wide
    gram_matrix = jnp.dot(hess_image.astype(jnp.float32), hess_image.T.astype(jnp.float32), precision=lax.Precision.HIGHEST, preferred_element_type=jnp.float32) / CELLS
    gram_matrix = gram_matrix + JITTER * jnp.eye(K, dtype=jnp.float32)
    lower_factor = jnp.linalg.cholesky(gram_matrix)
    basis_rows = jax.scipy.linalg.solve_triangular(lower_factor, hess_image, lower=True)
    return (basis_rows, lower_factor)
```

```python
import math

import jax
import jax.numpy as jnp
from jax import lax
from jax.sharding import Mesh, PartitionSpec as P

GRAVITY = 2.0
JITTER = 1e-06
SUBSTEP = 0.00390625
CELL_AXES = ("z", "yl", "x", "c")
NEAR = ("x", "c", "yh")
FAR = ("z", "yl")


def cell_points(cell_plan, cell_depth):
    cell_east = cell_plan[0].astype(jnp.float32) + 0.5
    cell_north = cell_plan[1].astype(jnp.float32) + 0.5
    cell_down = cell_depth.astype(jnp.float32) + 1.0
    return (cell_east, cell_north, cell_down)


def sensitivity(st_east, st_north, cell_geom):
    cell_east, cell_north, cell_down = cell_geom
    d_east = cell_east[None, :] - st_east[:, None]
    d_north = cell_north[None, :] - st_north[:, None]
    distance = d_east * d_east + d_north * d_north + cell_down[None, :] * cell_down[None, :]
    inverse = lax.rsqrt(distance)
    return (GRAVITY * cell_down[None, :] * inverse * inverse * inverse).astype(jnp.bfloat16)


def forward_terms(probes, st_east, st_north, cell_geom):
    station_count = st_east.shape[0]
    block_size = math.gcd(station_count, 512)

    def forward_advance(turn_index, running):
        start_at = turn_index * block_size
        sens_tile = sensitivity(
            lax.dynamic_slice_in_dim(st_east, start_at, block_size),
            lax.dynamic_slice_in_dim(st_north, start_at, block_size),
            cell_geom,
        )
        partial_value = lax.dot_general(
            probes, sens_tile, (((1,), (1,)), ((), ())), preferred_element_type=jnp.float32
        )
        return lax.dynamic_update_slice_in_dim(running, partial_value, start_at, 1)

    zero_field = jnp.zeros((probes.shape[0], station_count), jnp.float32)
    return lax.fori_loop(0, station_count // block_size, forward_advance, zero_field)


def transposed_add(running, weighted, st_east, st_north, cell_geom):
    station_count = weighted.shape[1]
    block_size = math.gcd(station_count, 512)

    def transposed_advance(turn_index, current):
        start_at = turn_index * block_size
        sens_tile = sensitivity(
            lax.dynamic_slice_in_dim(st_east, start_at, block_size),
            lax.dynamic_slice_in_dim(st_north, start_at, block_size),
            cell_geom,
        )
        segment = lax.dynamic_slice_in_dim(weighted, start_at, block_size, 1)
        return current + jnp.dot(segment, sens_tile, preferred_element_type=jnp.float32)

    return lax.fori_loop(0, station_count // block_size, transposed_advance, running)


def gram_term(hess_image):
    return jnp.dot(
        hess_image,
        hess_image.T,
        precision=lax.Precision.HIGHEST,
        preferred_element_type=jnp.float32,
    )


def exchanged(blocks, axes):
    return lax.all_to_all(blocks, axes, 0, 0, tiled=True)


def group_sum(value, axes):
    copies = jnp.broadcast_to(value[None], (lax.axis_size(axes), *value.shape))
    return jnp.sum(exchanged(copies, axes), axis=0)


def body(probes, reg_weight, cell_plan, cell_depth, station_index, station_weight):
    cell_geom = cell_points(cell_plan, cell_depth)
    st_east = station_index[0].astype(jnp.float32) * SUBSTEP
    st_north = station_index[1].astype(jnp.float32) * SUBSTEP
    station_scale = station_weight * station_weight
    terms = forward_terms(probes, st_east, st_north, cell_geom)
    blocks = terms.reshape(2, 2, 4, 32, 128).transpose(0, 3, 1, 2, 4).reshape(128, 4, 128)
    own_field = jnp.sum(exchanged(blocks, CELL_AXES), axis=0)
    own_block = (lax.axis_index(CELL_AXES) % 64) // 2
    own_scale = lax.dynamic_slice_in_dim(station_scale, own_block * 128, 128)
    own_weighted = (own_scale[None, :] * own_field).astype(jnp.bfloat16)
    gathered = exchanged(jnp.broadcast_to(own_weighted[None], (128, 4, 128)), CELL_AXES)
    weighted = gathered.reshape(2, 32, 2, 4, 128).transpose(0, 2, 3, 1, 4).reshape(16, 4096)
    zero_image = jnp.zeros((probes.shape[0], probes.shape[1]), jnp.float32)
    backward = transposed_add(zero_image, weighted, st_east, st_north, cell_geom)
    group_count = lax.axis_size("yh")
    quarter = probes.shape[1] // group_count
    offset_cells = lax.axis_index("yh") * quarter
    cell_total = probes.shape[1] * lax.axis_size(CELL_AXES)
    parts = backward.reshape(16, group_count, quarter).transpose(1, 0, 2)
    summed = jnp.sum(exchanged(parts, "yh"), axis=0)
    own_reg = lax.dynamic_slice_in_dim(reg_weight, offset_cells, quarter)
    own_probes = lax.dynamic_slice_in_dim(probes, offset_cells, quarter, 1)
    local_image = summed + own_reg[None, :] * own_probes.astype(jnp.float32)
    gram_flat = gram_term(local_image).reshape(2, 128)
    gram_flat = group_sum(group_sum(gram_flat, NEAR), FAR)
    gram_matrix = gram_flat.reshape(16, 16)
    gram_matrix = gram_matrix / cell_total + JITTER * jnp.eye(probes.shape[0], dtype=jnp.float32)
    lower_factor = jnp.linalg.cholesky(gram_matrix)
    basis_rows = jax.scipy.linalg.solve_triangular(lower_factor, local_image, lower=True)
    return (basis_rows, lower_factor)


def solution(mesh):
    split = Mesh(mesh.devices.reshape(8, 2, 4, 2, 4), ("z", "yl", "x", "c", "yh"))
    return jax.shard_map(
        body,
        mesh=split,
        in_specs=(
            P(None, CELL_AXES),
            P(CELL_AXES),
            P(None, CELL_AXES),
            P(CELL_AXES),
            P(None, "yh"),
            P("yh"),
        ),
        out_specs=(P(None, (*CELL_AXES, "yh")), P()),
        check_vma=False,
    )
```

```python
import functools
import math

import jax
import jax.numpy as jnp
from jax import lax
from jax.experimental import pallas as pl
from jax.experimental.pallas import tpu as pltpu
from jax.sharding import Mesh, PartitionSpec as P

GRAVITY = 2.0
JITTER = 1e-06
SUBSTEP = 0.00390625
K = 16
CELL_AXES = ("z", "yl", "x", "c")
SCATTER = ("yl", "x", "c")
REDUCE = ("z",)
NEAR = ("x", "c", "yh")
FAR = ("z", "yl")
SPAN = 1024
VMEM = pl.BlockSpec(memory_space=pltpu.VMEM)


def cell_points(cell_plan, cell_depth):
    cell_east = cell_plan[0].astype(jnp.float32) + 0.5
    cell_north = cell_plan[1].astype(jnp.float32) + 0.5
    cell_down = cell_depth.astype(jnp.float32) + 1.0
    return (cell_east, cell_north, cell_down)


def sensitivity(st_east, st_north, cell_geom):
    cell_east, cell_north, cell_down = cell_geom
    d_east = cell_east[None, :] - st_east[:, None]
    d_north = cell_north[None, :] - st_north[:, None]
    distance = d_east * d_east + d_north * d_north + cell_down[None, :] * cell_down[None, :]
    inverse = lax.rsqrt(distance)
    return (GRAVITY * cell_down[None, :] * inverse * inverse * inverse).astype(jnp.bfloat16)


def forward_terms(probes, st_east, st_north, cell_geom):
    station_count = st_east.shape[0]
    block_size = math.gcd(station_count, 512)

    def forward_advance(turn_index, running):
        start_at = turn_index * block_size
        sens_tile = sensitivity(
            lax.dynamic_slice_in_dim(st_east, start_at, block_size),
            lax.dynamic_slice_in_dim(st_north, start_at, block_size),
            cell_geom,
        )
        partial_value = lax.dot_general(
            probes, sens_tile, (((1,), (1,)), ((), ())), preferred_element_type=jnp.float32
        )
        return lax.dynamic_update_slice_in_dim(running, partial_value, start_at, 1)

    zero_field = jnp.zeros((probes.shape[0], station_count), jnp.float32)
    return lax.fori_loop(0, station_count // block_size, forward_advance, zero_field)


def transposed_add(running, weighted, st_east, st_north, cell_geom):
    station_count = weighted.shape[1]
    block_size = math.gcd(station_count, 512)

    def transposed_advance(turn_index, current):
        start_at = turn_index * block_size
        sens_tile = sensitivity(
            lax.dynamic_slice_in_dim(st_east, start_at, block_size),
            lax.dynamic_slice_in_dim(st_north, start_at, block_size),
            cell_geom,
        )
        segment = lax.dynamic_slice_in_dim(weighted, start_at, block_size, 1)
        return current + jnp.dot(segment, sens_tile, preferred_element_type=jnp.float32)

    return lax.fori_loop(0, station_count // block_size, transposed_advance, running)


def exchanged(blocks, axes):
    return lax.all_to_all(blocks, axes, 0, 0, tiled=True)


def called(kernel, name, out_shape, count, limit=8 << 20):
    outs = VMEM if not isinstance(out_shape, tuple) else (VMEM,) * len(out_shape)
    return pl.pallas_call(
        kernel,
        out_shape=out_shape,
        in_specs=[VMEM] * count,
        out_specs=outs,
        compiler_params=pltpu.CompilerParams(vmem_limit_bytes=limit),
        name=name,
    )


def sum_of(ref):
    total = ref[0]
    for i in range(1, ref.shape[0]):
        total = total + ref[i]
    return total


def copies_kernel(parts_ref, copies_ref):
    total = sum_of(parts_ref)
    for i in range(copies_ref.shape[0]):
        copies_ref[i] = total


def weigh_kernel(parts_ref, weight_ref, copies_ref):
    weight = weight_ref[...]
    total = ((weight * weight) * sum_of(parts_ref)).astype(jnp.bfloat16)
    for i in range(copies_ref.shape[0]):
        copies_ref[i] = total


def gram_kernel(parts_ref, reg_ref, probes_ref, image_ref, copies_ref):
    image = sum_of(parts_ref) + reg_ref[...] * probes_ref[...].astype(jnp.float32)
    image_ref[...] = image
    wide = lax.dot_general(
        image,
        jnp.concatenate([image] * 8, axis=0),
        (((1,), (1,)), ((), ())),
        precision=lax.Precision.HIGHEST,
        preferred_element_type=jnp.float32,
    )
    sub = lax.broadcasted_iota(jnp.int32, (K, 128), 0)
    lane = lax.broadcasted_iota(jnp.int32, (K, 128), 1)
    kept = jnp.where(lane // K == sub % 8, wide, 0.0)
    for half in range(2):
        packed = jnp.sum(kept[half * 8 : (half + 1) * 8, :], axis=0, keepdims=True)
        for i in range(copies_ref.shape[0]):
            copies_ref[i, half : half + 1, :] = packed


def solve_kernel(cell_total, parts_ref, image_ref, basis_ref, factor_ref):
    packed = sum_of(parts_ref)
    sub = lax.broadcasted_iota(jnp.int32, (K, 128), 0)
    lane = lax.broadcasted_iota(jnp.int32, (K, 128), 1)
    rows = jnp.concatenate([jnp.broadcast_to(packed[h : h + 1, :], (8, 128)) for h in range(2)], axis=0)
    rows = jnp.where(lane // K == sub % 8, rows, 0.0)
    for shift in (16, 32, 64):
        rows = rows + pltpu.roll(rows, shift, 1)
    matrix = rows / cell_total + jnp.where(lane == sub, JITTER, 0.0)
    right = image_ref[...]
    lower = jnp.zeros((K, 128), jnp.float32)
    for j in range(K):
        pivot = jnp.broadcast_to(matrix[j : j + 1, j : j + 1], (1, 128))
        scale = lax.rsqrt(pivot)
        scale = scale * (1.5 - 0.5 * pivot * scale * scale)
        column = jnp.where(sub >= j, jnp.broadcast_to(matrix[:, j : j + 1], (K, 128)) * scale, 0.0)
        lower = jnp.where(lane == j, column, lower)
        row = matrix[j : j + 1, :] * scale
        right_row = right[j : j + 1, :] * scale[:, 0:1]
        basis_ref[j : j + 1, :] = right_row
        if j + 1 < K:
            matrix = matrix - column * row
            right = right - column[:, 0:1] * right_row
    factor_ref[...] = lower[:, 0:K]


def body(probes, reg_weight, cell_plan, cell_depth, station_index, station_weight):
    f32 = jnp.float32
    cell_geom = cell_points(cell_plan, cell_depth)
    st_east = station_index[0].astype(f32) * SUBSTEP
    st_north = station_index[1].astype(f32) * SUBSTEP
    cells, stations = probes.shape[1], station_index.shape[1]
    terms = forward_terms(probes, st_east, st_north, cell_geom)
    blocks = lax.axis_size(SCATTER)
    across = blocks // 2
    width = stations // across
    field = terms.reshape(2, 8, across, width).transpose(0, 2, 1, 3).reshape(blocks, 8, width)
    parts = exchanged(field, SCATTER)
    count = lax.axis_size(REDUCE)
    parts = called(copies_kernel, "reduced", jax.ShapeDtypeStruct((count, 8, width), f32), 1)(parts)
    parts = exchanged(parts, REDUCE)
    start = (lax.axis_index(SCATTER) % across) * width
    own_weight = lax.dynamic_slice_in_dim(station_weight, start, width).reshape(1, width)
    own = called(weigh_kernel, "weighed", jax.ShapeDtypeStruct((blocks, 8, width), jnp.bfloat16), 2)(parts, own_weight)
    gathered = exchanged(own, SCATTER)
    weighted = gathered.reshape(2, across, 8, width).transpose(0, 2, 1, 3).reshape(K, stations)
    backward = transposed_add(jnp.zeros((K, cells), f32), weighted, st_east, st_north, cell_geom)
    parts = exchanged(backward.reshape(K, cells // SPAN, SPAN).transpose(1, 0, 2), "yh")
    offset = lax.axis_index("yh") * SPAN
    own_reg = lax.dynamic_slice_in_dim(reg_weight, offset, SPAN).reshape(1, SPAN)
    own_probes = lax.dynamic_slice_in_dim(probes, offset, SPAN, 1)
    near, far = lax.axis_size(NEAR), lax.axis_size(FAR)
    image, grams = called(
        gram_kernel,
        "gram",
        (jax.ShapeDtypeStruct((K, SPAN), f32), jax.ShapeDtypeStruct((near, 2, 128), f32)),
        3,
    )(parts, own_reg, own_probes)
    grams = called(copies_kernel, "summed", jax.ShapeDtypeStruct((far, 2, 128), f32), 1)(exchanged(grams, NEAR))
    cell_total = float(cells * lax.axis_size(CELL_AXES))
    return called(
        functools.partial(solve_kernel, cell_total),
        "solve",
        (jax.ShapeDtypeStruct((K, SPAN), f32), jax.ShapeDtypeStruct((K, K), f32)),
        2,
    )(exchanged(grams, FAR), image)


def solution(mesh):
    split = Mesh(mesh.devices.reshape(8, 2, 4, 2, 4), ("z", "yl", "x", "c", "yh"))
    return jax.shard_map(
        body,
        mesh=split,
        in_specs=(
            P(None, CELL_AXES),
            P(CELL_AXES),
            P(None, CELL_AXES),
            P(CELL_AXES),
            P(None, "yh"),
            P("yh"),
        ),
        out_specs=(P(None, (*CELL_AXES, "yh")), P()),
        check_vma=False,
    )
```

```python
import functools

import jax
import jax.numpy as jnp
from jax import lax
from jax.experimental import pallas as pl
from jax.experimental.pallas import tpu as pltpu
from jax.sharding import Mesh, PartitionSpec as P

GRAVITY = 2.0
JITTER = 1e-06
SUBSTEP = 0.00390625
K = 16
CELL_AXES = ("z", "yl", "x", "c")
SCATTER = ("yl", "x", "c")
REDUCE = ("z",)
NEAR = ("yl", "x", "c", "yh")
FAR = ("z",)
SPAN = 1024
VMEM = pl.BlockSpec(memory_space=pltpu.VMEM)


def sensitivity(st_east, st_north, cell_geom):
    cell_east, cell_north, down_squared, down_scaled = cell_geom
    d_east = cell_east - st_east[:, None]
    d_north = cell_north - st_north[:, None]
    inverse = lax.rsqrt(d_east * d_east + d_north * d_north + down_squared)
    return (down_scaled * inverse * inverse * inverse).astype(jnp.bfloat16)


def exchanged(blocks, axes):
    return lax.all_to_all(blocks, axes, 0, 0, tiled=True)


def called(kernel, name, out_shape, count, limit=8 << 20):
    outs = VMEM if not isinstance(out_shape, tuple) else (VMEM,) * len(out_shape)
    return pl.pallas_call(
        kernel,
        out_shape=out_shape,
        in_specs=[VMEM] * count,
        out_specs=outs,
        compiler_params=pltpu.CompilerParams(vmem_limit_bytes=limit),
        name=name,
    )


def geometry_kernel(plan_ref, depth_ref, station_ref, east_ref, north_ref, squared_ref, scaled_ref, st_east_ref, st_north_ref):
    east_ref[...] = plan_ref[0:1, :].astype(jnp.float32) + 0.5
    north_ref[...] = plan_ref[1:2, :].astype(jnp.float32) + 0.5
    for i in range(depth_ref.shape[0]):
        lanes = slice(i * 128, (i + 1) * 128)
        down = depth_ref[i : i + 1, :].astype(jnp.float32) + 1.0
        squared_ref[0:1, lanes] = down * down
        scaled_ref[0:1, lanes] = GRAVITY * down
    for i in range(st_east_ref.shape[0]):
        lanes = slice(i * 128, (i + 1) * 128)
        st_east_ref[i : i + 1, :] = station_ref[0:1, lanes].astype(jnp.float32) * SUBSTEP
        st_north_ref[i : i + 1, :] = station_ref[1:2, lanes].astype(jnp.float32) * SUBSTEP


def sum_of(ref):
    total = ref[0]
    for i in range(1, ref.shape[0]):
        total = total + ref[i]
    return total


def copies_kernel(parts_ref, copies_ref):
    total = sum_of(parts_ref)
    for i in range(copies_ref.shape[0]):
        copies_ref[i] = total


def weigh_kernel(parts_ref, weight_ref, copies_ref):
    weight = weight_ref[...]
    total = ((weight * weight) * sum_of(parts_ref)).astype(jnp.bfloat16)
    for i in range(copies_ref.shape[0]):
        copies_ref[i] = total


def gram_kernel(parts_ref, reg_ref, probes_ref, image_ref, copies_ref):
    image = sum_of(parts_ref) + reg_ref[...] * probes_ref[...].astype(jnp.float32)
    image_ref[...] = image
    wide = lax.dot_general(
        image,
        jnp.concatenate([image] * 8, axis=0),
        (((1,), (1,)), ((), ())),
        precision=lax.Precision.HIGHEST,
        preferred_element_type=jnp.float32,
    )
    sub = lax.broadcasted_iota(jnp.int32, (K, 128), 0)
    lane = lax.broadcasted_iota(jnp.int32, (K, 128), 1)
    kept = jnp.where(lane // K == sub % 8, wide, 0.0)
    for half in range(2):
        packed = jnp.sum(kept[half * 8 : (half + 1) * 8, :], axis=0, keepdims=True)
        for i in range(copies_ref.shape[0]):
            copies_ref[i, half : half + 1, :] = packed


def solve_kernel(cell_total, parts_ref, image_ref, basis_ref, factor_ref):
    packed = sum_of(parts_ref)
    sub = lax.broadcasted_iota(jnp.int32, (K, 128), 0)
    lane = lax.broadcasted_iota(jnp.int32, (K, 128), 1)
    rows = jnp.concatenate([jnp.broadcast_to(packed[h : h + 1, :], (8, 128)) for h in range(2)], axis=0)
    rows = jnp.where(lane // K == sub % 8, rows, 0.0)
    for shift in (16, 32, 64):
        rows = rows + pltpu.roll(rows, shift, 1)
    matrix = rows / cell_total + jnp.where(lane == sub, JITTER, 0.0)
    right = image_ref[...]
    lower = jnp.zeros((K, 128), jnp.float32)
    for j in range(K):
        pivot = jnp.broadcast_to(matrix[j : j + 1, j : j + 1], (1, 128))
        scale = lax.rsqrt(pivot)
        scale = scale * (1.5 - 0.5 * pivot * scale * scale)
        column = jnp.where(sub >= j, jnp.broadcast_to(matrix[:, j : j + 1], (K, 128)) * scale, 0.0)
        lower = jnp.where(lane == j, column, lower)
        row = matrix[j : j + 1, :] * scale
        right_row = right[j : j + 1, :] * scale[:, 0:1]
        basis_ref[j : j + 1, :] = right_row
        if j + 1 < K:
            matrix = matrix - column * row
            right = right - column[:, 0:1] * right_row
    factor_ref[...] = lower[:, 0:K]


def body(probes, reg_weight, cell_plan, cell_depth, station_index, station_weight):
    f32 = jnp.float32
    cells, stations = probes.shape[1], station_index.shape[1]
    row = jax.ShapeDtypeStruct((1, cells), f32)
    tiles = jax.ShapeDtypeStruct((stations // 128, 128), f32)
    geometry = called(geometry_kernel, "geometry", (row, row, row, row, tiles, tiles), 3)
    *cell_geom, st_east, st_north = geometry(cell_plan, cell_depth.reshape(-1, 128), station_index)
    st_east, st_north = st_east.reshape(stations), st_north.reshape(stations)
    terms = lax.dot_general(
        probes,
        sensitivity(st_east, st_north, cell_geom),
        (((1,), (1,)), ((), ())),
        preferred_element_type=f32,
    )
    blocks = lax.axis_size(SCATTER)
    across = blocks // 2
    width = stations // across
    field = terms.reshape(2, 8, across, width).transpose(0, 2, 1, 3).reshape(blocks, 8, width)
    parts = exchanged(field, SCATTER)
    count = lax.axis_size(REDUCE)
    parts = called(copies_kernel, "reduced", jax.ShapeDtypeStruct((count, 8, width), f32), 1)(parts)
    parts = exchanged(parts, REDUCE)
    start = (lax.axis_index(SCATTER) % across) * width
    own_weight = lax.dynamic_slice_in_dim(station_weight, start, width).reshape(1, width)
    own = called(weigh_kernel, "weighed", jax.ShapeDtypeStruct((blocks, 8, width), jnp.bfloat16), 2)(parts, own_weight)
    gathered = exchanged(own, SCATTER)
    weighted = gathered.reshape(2, across, 8, width).transpose(0, 2, 1, 3).reshape(K, stations)
    st_east, st_north, *cell_geom = lax.optimization_barrier((st_east, st_north, *cell_geom))
    backward = jnp.dot(weighted, sensitivity(st_east, st_north, cell_geom), preferred_element_type=f32)
    parts = exchanged(backward.reshape(K, cells // SPAN, SPAN).transpose(1, 0, 2), "yh")
    offset = lax.axis_index("yh") * SPAN
    own_reg = lax.dynamic_slice_in_dim(reg_weight, offset, SPAN).reshape(1, SPAN)
    own_probes = lax.dynamic_slice_in_dim(probes, offset, SPAN, 1)
    near, far = lax.axis_size(NEAR), lax.axis_size(FAR)
    image, grams = called(
        gram_kernel,
        "gram",
        (jax.ShapeDtypeStruct((K, SPAN), f32), jax.ShapeDtypeStruct((near, 2, 128), f32)),
        3,
    )(parts, own_reg, own_probes)
    grams = called(copies_kernel, "summed", jax.ShapeDtypeStruct((far, 2, 128), f32), 1)(exchanged(grams, NEAR))
    cell_total = float(cells * lax.axis_size(CELL_AXES))
    return called(
        functools.partial(solve_kernel, cell_total),
        "solve",
        (jax.ShapeDtypeStruct((K, SPAN), f32), jax.ShapeDtypeStruct((K, K), f32)),
        2,
    )(exchanged(grams, FAR), image)


def solution(mesh):
    split = Mesh(mesh.devices.reshape(8, 2, 4, 2, 4), ("z", "yl", "x", "c", "yh"))
    return jax.shard_map(
        body,
        mesh=split,
        in_specs=(
            P(None, CELL_AXES),
            P(CELL_AXES),
            P(None, CELL_AXES),
            P(CELL_AXES),
            P(None, "yh"),
            P("yh"),
        ),
        out_specs=(P(None, (*CELL_AXES, "yh")), P()),
        check_vma=False,
    )
```

```python
import functools

import jax
import jax.numpy as jnp
from jax import lax
from jax.experimental import pallas as pl
from jax.experimental.pallas import tpu as pltpu
from jax.sharding import Mesh, PartitionSpec as P

GRAVITY = 2.0
JITTER = 1e-06
SUBSTEP = 0.00390625
K = 16
CELL_AXES = ("z", "yl", "x", "c")
SCATTER = ("yl", "x", "c")
REDUCE = ("z",)
NEAR = ("yl", "c", "yh")
FAR = ("z", "x")
SPAN = 1024
FILLS = (1024, 512, 512)
VMEM = pl.BlockSpec(memory_space=pltpu.VMEM)


def sensitivity(st_east, st_north, cell_geom):
    cell_east, cell_north, down_squared, down_scaled = cell_geom
    d_east = cell_east - st_east[:, None]
    d_north = cell_north - st_north[:, None]
    inverse = lax.rsqrt(d_east * d_east + d_north * d_north + down_squared)
    return (down_scaled * inverse * inverse * inverse).astype(jnp.bfloat16)


def exchanged(blocks, axes):
    return lax.all_to_all(blocks, axes, 0, 0, tiled=True)


def called(kernel, name, out_shape, count, limit=8 << 20):
    outs = VMEM if not isinstance(out_shape, tuple) else (VMEM,) * len(out_shape)
    return pl.pallas_call(
        kernel,
        out_shape=out_shape,
        in_specs=[VMEM] * count,
        out_specs=outs,
        compiler_params=pltpu.CompilerParams(vmem_limit_bytes=limit),
        name=name,
    )


def geometry_kernel(plan_ref, depth_ref, station_ref, east_ref, north_ref, squared_ref, scaled_ref, st_east_ref, st_north_ref):
    east_ref[...] = plan_ref[0:1, :].astype(jnp.float32) + 0.5
    north_ref[...] = plan_ref[1:2, :].astype(jnp.float32) + 0.5
    for i in range(depth_ref.shape[0]):
        lanes = slice(i * 128, (i + 1) * 128)
        down = depth_ref[i : i + 1, :].astype(jnp.float32) + 1.0
        squared_ref[0:1, lanes] = down * down
        scaled_ref[0:1, lanes] = GRAVITY * down
    for i in range(st_east_ref.shape[0]):
        lanes = slice(i * 128, (i + 1) * 128)
        st_east_ref[i : i + 1, :] = station_ref[0:1, lanes].astype(jnp.float32) * SUBSTEP
        st_north_ref[i : i + 1, :] = station_ref[1:2, lanes].astype(jnp.float32) * SUBSTEP


def sum_of(ref):
    total = ref[0]
    for i in range(1, ref.shape[0]):
        total = total + ref[i]
    return total


def copies_kernel(parts_ref, copies_ref):
    total = sum_of(parts_ref)
    for i in range(copies_ref.shape[0]):
        copies_ref[i] = total


def weigh_kernel(parts_ref, weight_ref, copies_ref):
    weight = weight_ref[...]
    total = ((weight * weight) * sum_of(parts_ref)).astype(jnp.bfloat16)
    for i in range(copies_ref.shape[0]):
        copies_ref[i] = total


def gram_kernel(parts_ref, reg_ref, probes_ref, image_ref, copies_ref):
    image = sum_of(parts_ref) + reg_ref[...] * probes_ref[...].astype(jnp.float32)
    image_ref[...] = image
    wide = lax.dot_general(
        image,
        jnp.concatenate([image] * 8, axis=0),
        (((1,), (1,)), ((), ())),
        precision=lax.Precision.HIGHEST,
        preferred_element_type=jnp.float32,
    )
    sub = lax.broadcasted_iota(jnp.int32, (K, 128), 0)
    lane = lax.broadcasted_iota(jnp.int32, (K, 128), 1)
    kept = jnp.where(lane // K == sub % 8, wide, 0.0)
    for half in range(2):
        packed = jnp.sum(kept[half * 8 : (half + 1) * 8, :], axis=0, keepdims=True)
        for i in range(copies_ref.shape[0]):
            copies_ref[i, half : half + 1, :] = packed


def solve_kernel(cell_total, parts_ref, image_ref, basis_ref, factor_ref):
    packed = sum_of(parts_ref)
    sub = lax.broadcasted_iota(jnp.int32, (K, 128), 0)
    lane = lax.broadcasted_iota(jnp.int32, (K, 128), 1)
    rows = jnp.concatenate([jnp.broadcast_to(packed[h : h + 1, :], (8, 128)) for h in range(2)], axis=0)
    rows = jnp.where(lane // K == sub % 8, rows, 0.0)
    for shift in (16, 32, 64):
        rows = rows + pltpu.roll(rows, shift, 1)
    matrix = rows / cell_total + jnp.where(lane == sub, JITTER, 0.0)
    right = image_ref[...]
    lower = jnp.zeros((K, 128), jnp.float32)
    for j in range(K):
        pivot = jnp.broadcast_to(matrix[j : j + 1, j : j + 1], (1, 128))
        scale = lax.rsqrt(pivot)
        scale = scale * (1.5 - 0.5 * pivot * scale * scale)
        column = jnp.where(sub >= j, jnp.broadcast_to(matrix[:, j : j + 1], (K, 128)) * scale, 0.0)
        lower = jnp.where(lane == j, column, lower)
        row = matrix[j : j + 1, :] * scale
        right_row = right[j : j + 1, :] * scale[:, 0:1]
        basis_ref[j : j + 1, :] = right_row
        if j + 1 < K:
            matrix = matrix - column * row
            right = right - column[:, 0:1] * right_row
    factor_ref[...] = lower[:, 0:K]


def body(probes, reg_weight, cell_plan, cell_depth, station_index, station_weight):
    f32 = jnp.float32
    cells, stations = probes.shape[1], station_index.shape[1]
    row = jax.ShapeDtypeStruct((1, cells), f32)
    tiles = jax.ShapeDtypeStruct((stations // 128, 128), f32)
    sources = (cell_plan, cell_depth.reshape(-1, 128), station_index)
    *cell_geom, st_east, st_north = pl.pallas_call(
        geometry_kernel,
        grid=(1,),
        out_shape=(row, row, row, row, tiles, tiles),
        in_specs=[pl.BlockSpec(source.shape, lambda i: (0, 0)) for source in sources],
        out_specs=(VMEM,) * 6,
        compiler_params=pltpu.CompilerParams(vmem_limit_bytes=8 << 20),
        name="geometry",
    )(*sources)
    st_east, st_north = st_east.reshape(stations), st_north.reshape(stations)
    terms = lax.dot_general(
        probes,
        sensitivity(st_east, st_north, cell_geom),
        (((1,), (1,)), ((), ())),
        preferred_element_type=f32,
    )
    ends = [sum(FILLS[: i + 1]) for i in range(len(FILLS))]

    def kept(i, geometry):
        here = slice(ends[i] - FILLS[i], ends[i])
        st_east, st_north, *cell_geom = geometry
        return sensitivity(st_east[here], st_north[here], cell_geom)

    geometry = (st_east, st_north, *cell_geom)
    blocks = lax.axis_size(SCATTER)
    across = blocks // 2
    width = stations // across
    field = terms.reshape(2, 8, across, width).transpose(0, 2, 1, 3).reshape(blocks, 8, width)
    field, geometry = lax.optimization_barrier((field, geometry))
    parts, first = lax.optimization_barrier((exchanged(field, SCATTER), kept(0, geometry)))
    count = lax.axis_size(REDUCE)
    parts = called(copies_kernel, "reduced", jax.ShapeDtypeStruct((count, 8, width), f32), 1)(parts)
    parts, geometry = lax.optimization_barrier((parts, geometry))
    parts, second = lax.optimization_barrier((exchanged(parts, REDUCE), kept(1, geometry)))
    start = (lax.axis_index(SCATTER) % across) * width
    own_weight = lax.dynamic_slice_in_dim(station_weight, start, width).reshape(1, width)
    own = called(weigh_kernel, "weighed", jax.ShapeDtypeStruct((blocks, 8, width), jnp.bfloat16), 2)(parts, own_weight)
    own, geometry = lax.optimization_barrier((own, geometry))
    gathered, third = lax.optimization_barrier((exchanged(own, SCATTER), kept(2, geometry)))
    weighted = gathered.reshape(2, across, 8, width).transpose(0, 2, 1, 3).reshape(K, stations)
    backward = jnp.dot(
        weighted[:, ends[-1] :],
        sensitivity(geometry[0][ends[-1] :], geometry[1][ends[-1] :], geometry[2:]),
        preferred_element_type=f32,
    )
    for i, sens in enumerate((first, second, third)):
        segment = weighted[:, ends[i] - FILLS[i] : ends[i]]
        backward = backward + jnp.dot(segment, sens, preferred_element_type=f32)
    parts = exchanged(backward.reshape(K, cells // SPAN, SPAN).transpose(1, 0, 2), "yh")
    offset = lax.axis_index("yh") * SPAN
    own_reg = lax.dynamic_slice_in_dim(reg_weight, offset, SPAN).reshape(1, SPAN)
    own_probes = lax.dynamic_slice_in_dim(probes, offset, SPAN, 1)
    near, far = lax.axis_size(NEAR), lax.axis_size(FAR)
    image, grams = called(
        gram_kernel,
        "gram",
        (jax.ShapeDtypeStruct((K, SPAN), f32), jax.ShapeDtypeStruct((near, 2, 128), f32)),
        3,
    )(parts, own_reg, own_probes)
    grams = called(copies_kernel, "summed", jax.ShapeDtypeStruct((far, 2, 128), f32), 1)(exchanged(grams, NEAR))
    cell_total = float(cells * lax.axis_size(CELL_AXES))
    return called(
        functools.partial(solve_kernel, cell_total),
        "solve",
        (jax.ShapeDtypeStruct((K, SPAN), f32), jax.ShapeDtypeStruct((K, K), f32)),
        2,
    )(exchanged(grams, FAR), image)


def solution(mesh):
    split = Mesh(mesh.devices.reshape(8, 2, 4, 2, 4), ("z", "yl", "x", "c", "yh"))
    return jax.shard_map(
        body,
        mesh=split,
        in_specs=(
            P(None, CELL_AXES),
            P(CELL_AXES),
            P(None, CELL_AXES),
            P(CELL_AXES),
            P(None, "yh"),
            P("yh"),
        ),
        out_specs=(P(None, (*CELL_AXES, "yh")), P()),
        check_vma=False,
    )
```

```python
import functools

import jax
import jax.numpy as jnp
from jax import lax
from jax.experimental import pallas as pl
from jax.experimental.pallas import tpu as pltpu
from jax.sharding import Mesh, PartitionSpec as P

GRAVITY = 2.0
JITTER = 1e-06
SUBSTEP = 0.00390625
K = 16
CELL_AXES = ("z", "yl", "x", "c")
SCATTER = ("yl", "x", "c")
REDUCE = ("z",)
NEAR = ("yl", "c", "yh")
FAR = ("z", "x")
SPAN = 1024
FILL = 512
VMEM = pl.BlockSpec(memory_space=pltpu.VMEM)


def sensitivity(st_east, st_north, cell_geom):
    cell_east, cell_north, down_squared, down_scaled = cell_geom
    d_east = cell_east - st_east[:, None]
    d_north = cell_north - st_north[:, None]
    inverse = lax.rsqrt(d_east * d_east + d_north * d_north + down_squared)
    return (down_scaled * inverse * inverse * inverse).astype(jnp.bfloat16)


def exchanged(blocks, axes):
    return lax.all_to_all(blocks, axes, 0, 0, tiled=True)


def called(kernel, name, out_shape, count, limit=8 << 20):
    outs = VMEM if not isinstance(out_shape, tuple) else (VMEM,) * len(out_shape)
    return pl.pallas_call(
        kernel,
        out_shape=out_shape,
        in_specs=[VMEM] * count,
        out_specs=outs,
        compiler_params=pltpu.CompilerParams(vmem_limit_bytes=limit),
        name=name,
    )


def geometry_kernel(plan_ref, depth_ref, station_ref, east_ref, north_ref, squared_ref, scaled_ref, st_east_ref, st_north_ref):
    east_ref[...] = plan_ref[0:1, :].astype(jnp.float32) + 0.5
    north_ref[...] = plan_ref[1:2, :].astype(jnp.float32) + 0.5
    for i in range(depth_ref.shape[0]):
        lanes = slice(i * 128, (i + 1) * 128)
        down = depth_ref[i : i + 1, :].astype(jnp.float32) + 1.0
        squared_ref[0:1, lanes] = down * down
        scaled_ref[0:1, lanes] = GRAVITY * down
    for i in range(st_east_ref.shape[0]):
        lanes = slice(i * 128, (i + 1) * 128)
        st_east_ref[i : i + 1, :] = station_ref[0:1, lanes].astype(jnp.float32) * SUBSTEP
        st_north_ref[i : i + 1, :] = station_ref[1:2, lanes].astype(jnp.float32) * SUBSTEP


def kept_kernel(first, east_ref, north_ref, squared_ref, scaled_ref, st_east_ref, st_north_ref, sens_ref, se_ref, sn_ref):
    tile = first // 128 + pl.program_id(0)
    se_ref[...] = jnp.broadcast_to(st_east_ref[pl.ds(tile, 1), :], (128, 128)).T
    sn_ref[...] = jnp.broadcast_to(st_north_ref[pl.ds(tile, 1), :], (128, 128)).T

    def span(g, carry):
        for t in range(2 * SPAN // 128):
            lanes = pl.ds(pl.multiple_of(g * 2 * SPAN + t * 128, 128), 128)
            cell_rows = (east_ref, north_ref, squared_ref, scaled_ref)
            ce, cn, dd, td = [jnp.broadcast_to(ref[0:1, lanes], (16, 128)) for ref in cell_rows]
            for r in range(8):
                subs = slice(r * 16, (r + 1) * 16)
                d_east = ce - se_ref[subs, :]
                d_north = cn - sn_ref[subs, :]
                inverse = lax.rsqrt(d_east * d_east + d_north * d_north + dd)
                sens_ref[subs, lanes] = (td * inverse * inverse * inverse).astype(jnp.bfloat16)
        return carry

    lax.fori_loop(0, sens_ref.shape[1] // (2 * SPAN), span, 0)


def kept(first, geometry):
    cells = geometry[0].shape[1]
    return pl.pallas_call(
        functools.partial(kept_kernel, first),
        grid=(FILL // 128,),
        out_shape=pltpu.HBM((FILL, cells), jnp.bfloat16),
        in_specs=[VMEM] * 6,
        out_specs=pl.BlockSpec((128, cells), lambda b: (b, 0)),
        scratch_shapes=[pltpu.VMEM((128, 128), jnp.float32), pltpu.VMEM((128, 128), jnp.float32)],
        cost_estimate=pl.CostEstimate(
            flops=10 * FILL * cells, transcendentals=FILL * cells, bytes_accessed=2 * FILL * cells
        ),
        compiler_params=pltpu.CompilerParams(vmem_limit_bytes=8 << 20),
        name="kept",
    )(*geometry)


def sum_of(ref):
    total = ref[0]
    for i in range(1, ref.shape[0]):
        total = total + ref[i]
    return total


def copies_kernel(parts_ref, copies_ref):
    total = sum_of(parts_ref)
    for i in range(copies_ref.shape[0]):
        copies_ref[i] = total


def weigh_kernel(parts_ref, weight_ref, copies_ref):
    weight = weight_ref[...]
    total = ((weight * weight) * sum_of(parts_ref)).astype(jnp.bfloat16)
    for i in range(copies_ref.shape[0]):
        copies_ref[i] = total


def gram_kernel(parts_ref, reg_ref, probes_ref, image_ref, copies_ref):
    image = sum_of(parts_ref) + reg_ref[...] * probes_ref[...].astype(jnp.float32)
    image_ref[...] = image
    wide = lax.dot_general(
        image,
        jnp.concatenate([image] * 8, axis=0),
        (((1,), (1,)), ((), ())),
        precision=lax.Precision.HIGHEST,
        preferred_element_type=jnp.float32,
    )
    sub = lax.broadcasted_iota(jnp.int32, (K, 128), 0)
    lane = lax.broadcasted_iota(jnp.int32, (K, 128), 1)
    kept = jnp.where(lane // K == sub % 8, wide, 0.0)
    for half in range(2):
        packed = jnp.sum(kept[half * 8 : (half + 1) * 8, :], axis=0, keepdims=True)
        for i in range(copies_ref.shape[0]):
            copies_ref[i, half : half + 1, :] = packed


def solve_kernel(cell_total, parts_ref, image_ref, basis_ref, factor_ref):
    packed = sum_of(parts_ref)
    sub = lax.broadcasted_iota(jnp.int32, (K, 128), 0)
    lane = lax.broadcasted_iota(jnp.int32, (K, 128), 1)
    rows = jnp.concatenate([jnp.broadcast_to(packed[h : h + 1, :], (8, 128)) for h in range(2)], axis=0)
    rows = jnp.where(lane // K == sub % 8, rows, 0.0)
    for shift in (16, 32, 64):
        rows = rows + pltpu.roll(rows, shift, 1)
    matrix = rows / cell_total + jnp.where(lane == sub, JITTER, 0.0)
    right = image_ref[...]
    lower = jnp.zeros((K, 128), jnp.float32)
    for j in range(K):
        pivot = jnp.broadcast_to(matrix[j : j + 1, j : j + 1], (1, 128))
        scale = lax.rsqrt(pivot)
        scale = scale * (1.5 - 0.5 * pivot * scale * scale)
        column = jnp.where(sub >= j, jnp.broadcast_to(matrix[:, j : j + 1], (K, 128)) * scale, 0.0)
        lower = jnp.where(lane == j, column, lower)
        row = matrix[j : j + 1, :] * scale
        right_row = right[j : j + 1, :] * scale[:, 0:1]
        basis_ref[j : j + 1, :] = right_row
        if j + 1 < K:
            matrix = matrix - column * row
            right = right - column[:, 0:1] * right_row
    factor_ref[...] = lower[:, 0:K]


def body(probes, reg_weight, cell_plan, cell_depth, station_index, station_weight):
    f32 = jnp.float32
    cells, stations = probes.shape[1], station_index.shape[1]
    row = jax.ShapeDtypeStruct((1, cells), f32)
    tiles = jax.ShapeDtypeStruct((stations // 128, 128), f32)
    sources = (cell_plan, cell_depth.reshape(-1, 128), station_index)
    *cell_geom, tiles_east, tiles_north = pl.pallas_call(
        geometry_kernel,
        grid=(1,),
        out_shape=(row, row, row, row, tiles, tiles),
        in_specs=[pl.BlockSpec(source.shape, lambda i: (0, 0)) for source in sources],
        out_specs=(VMEM,) * 6,
        compiler_params=pltpu.CompilerParams(vmem_limit_bytes=8 << 20),
        name="geometry",
    )(*sources)
    st_east, st_north = tiles_east.reshape(stations), tiles_north.reshape(stations)
    terms = lax.dot_general(
        probes,
        sensitivity(st_east, st_north, cell_geom),
        (((1,), (1,)), ((), ())),
        preferred_element_type=f32,
    )
    geometry = (*cell_geom, tiles_east, tiles_north)
    blocks = lax.axis_size(SCATTER)
    across = blocks // 2
    width = stations // across
    field = terms.reshape(2, 8, across, width).transpose(0, 2, 1, 3).reshape(blocks, 8, width)
    field, geometry = lax.optimization_barrier((field, geometry))
    pieces = [kept(0, geometry), kept(FILL, geometry)]
    parts, pieces = lax.optimization_barrier((exchanged(field, SCATTER), pieces))
    count = lax.axis_size(REDUCE)
    parts = called(copies_kernel, "reduced", jax.ShapeDtypeStruct((count, 8, width), f32), 1)(parts)
    parts, geometry = lax.optimization_barrier((parts, geometry))
    parts, piece = lax.optimization_barrier((exchanged(parts, REDUCE), kept(2 * FILL, geometry)))
    pieces.append(piece)
    start = (lax.axis_index(SCATTER) % across) * width
    own_weight = lax.dynamic_slice_in_dim(station_weight, start, width).reshape(1, width)
    own = called(weigh_kernel, "weighed", jax.ShapeDtypeStruct((blocks, 8, width), jnp.bfloat16), 2)(parts, own_weight)
    own, geometry = lax.optimization_barrier((own, geometry))
    gathered, piece = lax.optimization_barrier((exchanged(own, SCATTER), kept(3 * FILL, geometry)))
    pieces.append(piece)
    weighted = gathered.reshape(2, across, 8, width).transpose(0, 2, 1, 3).reshape(K, stations)
    done = len(pieces) * FILL
    *cell_geom, tiles_east, tiles_north = geometry
    st_east, st_north = tiles_east.reshape(stations)[done:], tiles_north.reshape(stations)[done:]
    backward = jnp.dot(weighted[:, done:], sensitivity(st_east, st_north, cell_geom), preferred_element_type=f32)
    for i, sens in enumerate(pieces):
        segment = weighted[:, i * FILL : (i + 1) * FILL]
        backward = backward + jnp.dot(segment, sens, preferred_element_type=f32)
    parts = exchanged(backward.reshape(K, cells // SPAN, SPAN).transpose(1, 0, 2), "yh")
    offset = lax.axis_index("yh") * SPAN
    own_reg = lax.dynamic_slice_in_dim(reg_weight, offset, SPAN).reshape(1, SPAN)
    own_probes = lax.dynamic_slice_in_dim(probes, offset, SPAN, 1)
    near, far = lax.axis_size(NEAR), lax.axis_size(FAR)
    image, grams = called(
        gram_kernel,
        "gram",
        (jax.ShapeDtypeStruct((K, SPAN), f32), jax.ShapeDtypeStruct((near, 2, 128), f32)),
        3,
    )(parts, own_reg, own_probes)
    grams = called(copies_kernel, "summed", jax.ShapeDtypeStruct((far, 2, 128), f32), 1)(exchanged(grams, NEAR))
    cell_total = float(cells * lax.axis_size(CELL_AXES))
    return called(
        functools.partial(solve_kernel, cell_total),
        "solve",
        (jax.ShapeDtypeStruct((K, SPAN), f32), jax.ShapeDtypeStruct((K, K), f32)),
        2,
    )(exchanged(grams, FAR), image)


def solution(mesh):
    split = Mesh(mesh.devices.reshape(8, 2, 4, 2, 4), ("z", "yl", "x", "c", "yh"))
    return jax.shard_map(
        body,
        mesh=split,
        in_specs=(
            P(None, CELL_AXES),
            P(CELL_AXES),
            P(None, CELL_AXES),
            P(CELL_AXES),
            P(None, "yh"),
            P("yh"),
        ),
        out_specs=(P(None, (*CELL_AXES, "yh")), P()),
        check_vma=False,
    )
```

```python
import functools

import jax
import jax.numpy as jnp
from jax import lax
from jax.experimental import pallas as pl
from jax.experimental.pallas import tpu as pltpu
from jax.sharding import Mesh, PartitionSpec as P

GRAVITY = 2.0
JITTER = 1e-06
SUBSTEP = 0.00390625
K = 16
CELL_AXES = ("z", "yl", "x", "c")
SCATTER = ("yl", "x", "c")
REDUCE = ("z",)
NEAR = ("yl", "c", "yh")
FAR = ("z", "x")
SPAN = 1024
FILLS = (768, 512, 512)
VMEM = pl.BlockSpec(memory_space=pltpu.VMEM)


def sensitivity(st_east, st_north, cell_geom):
    cell_east, cell_north, down_squared, down_scaled = cell_geom
    d_east = cell_east - st_east[:, None]
    d_north = cell_north - st_north[:, None]
    inverse = lax.rsqrt(d_east * d_east + d_north * d_north + down_squared)
    return (down_scaled * inverse * inverse * inverse).astype(jnp.bfloat16)


def exchanged(blocks, axes):
    return lax.all_to_all(blocks, axes, 0, 0, tiled=True)


def called(kernel, name, out_shape, count, limit=8 << 20):
    outs = VMEM if not isinstance(out_shape, tuple) else (VMEM,) * len(out_shape)
    return pl.pallas_call(
        kernel,
        out_shape=out_shape,
        in_specs=[VMEM] * count,
        out_specs=outs,
        compiler_params=pltpu.CompilerParams(vmem_limit_bytes=limit),
        name=name,
    )


def geometry_kernel(plan_ref, depth_ref, station_ref, east_ref, north_ref, squared_ref, scaled_ref, st_east_ref, st_north_ref):
    east_ref[...] = plan_ref[0:1, :].astype(jnp.float32) + 0.5
    north_ref[...] = plan_ref[1:2, :].astype(jnp.float32) + 0.5
    for i in range(depth_ref.shape[0]):
        lanes = slice(i * 128, (i + 1) * 128)
        down = depth_ref[i : i + 1, :].astype(jnp.float32) + 1.0
        squared_ref[0:1, lanes] = down * down
        scaled_ref[0:1, lanes] = GRAVITY * down
    for i in range(st_east_ref.shape[0]):
        lanes = slice(i * 128, (i + 1) * 128)
        st_east_ref[i : i + 1, :] = station_ref[0:1, lanes].astype(jnp.float32) * SUBSTEP
        st_north_ref[i : i + 1, :] = station_ref[1:2, lanes].astype(jnp.float32) * SUBSTEP


def sum_of(ref):
    total = ref[0]
    for i in range(1, ref.shape[0]):
        total = total + ref[i]
    return total


def copies_kernel(parts_ref, copies_ref):
    total = sum_of(parts_ref)
    for i in range(copies_ref.shape[0]):
        copies_ref[i] = total


def weigh_kernel(parts_ref, weight_ref, copies_ref):
    weight = weight_ref[...]
    total = ((weight * weight) * sum_of(parts_ref)).astype(jnp.bfloat16)
    for i in range(copies_ref.shape[0]):
        copies_ref[i] = total


def gram_kernel(parts_ref, reg_ref, probes_ref, image_ref, copies_ref):
    image = sum_of(parts_ref) + reg_ref[...] * probes_ref[...].astype(jnp.float32)
    image_ref[...] = image
    wide = lax.dot_general(
        image,
        jnp.concatenate([image] * 8, axis=0),
        (((1,), (1,)), ((), ())),
        precision=lax.Precision.HIGHEST,
        preferred_element_type=jnp.float32,
    )
    sub = lax.broadcasted_iota(jnp.int32, (K, 128), 0)
    lane = lax.broadcasted_iota(jnp.int32, (K, 128), 1)
    kept = jnp.where(lane // K == sub % 8, wide, 0.0)
    for half in range(2):
        packed = jnp.sum(kept[half * 8 : (half + 1) * 8, :], axis=0, keepdims=True)
        for i in range(copies_ref.shape[0]):
            copies_ref[i, half : half + 1, :] = packed


def solve_kernel(cell_total, parts_ref, image_ref, basis_ref, factor_ref):
    packed = sum_of(parts_ref)
    sub = lax.broadcasted_iota(jnp.int32, (K, 128), 0)
    lane = lax.broadcasted_iota(jnp.int32, (K, 128), 1)
    rows = jnp.concatenate([jnp.broadcast_to(packed[h : h + 1, :], (8, 128)) for h in range(2)], axis=0)
    rows = jnp.where(lane // K == sub % 8, rows, 0.0)
    for shift in (16, 32, 64):
        rows = rows + pltpu.roll(rows, shift, 1)
    matrix = rows / cell_total + jnp.where(lane == sub, JITTER, 0.0)
    right = image_ref[...]
    lower = jnp.zeros((K, 128), jnp.float32)
    for j in range(K):
        pivot = jnp.broadcast_to(matrix[j : j + 1, j : j + 1], (1, 128))
        scale = lax.rsqrt(pivot)
        scale = scale * (1.5 - 0.5 * pivot * scale * scale)
        column = jnp.where(sub >= j, jnp.broadcast_to(matrix[:, j : j + 1], (K, 128)) * scale, 0.0)
        lower = jnp.where(lane == j, column, lower)
        row = matrix[j : j + 1, :] * scale
        right_row = right[j : j + 1, :] * scale[:, 0:1]
        basis_ref[j : j + 1, :] = right_row
        if j + 1 < K:
            matrix = matrix - column * row
            right = right - column[:, 0:1] * right_row
    factor_ref[...] = lower[:, 0:K]


def body(probes, reg_weight, cell_plan, cell_depth, station_index, station_weight):
    f32 = jnp.float32
    cells, stations = probes.shape[1], station_index.shape[1]
    row = jax.ShapeDtypeStruct((1, cells), f32)
    tiles = jax.ShapeDtypeStruct((stations // 128, 128), f32)
    sources = (cell_plan, cell_depth.reshape(-1, 128), station_index)
    *cell_geom, st_east, st_north = pl.pallas_call(
        geometry_kernel,
        grid=(1,),
        out_shape=(row, row, row, row, tiles, tiles),
        in_specs=[pl.BlockSpec(source.shape, lambda i: (0, 0)) for source in sources],
        out_specs=(VMEM,) * 6,
        compiler_params=pltpu.CompilerParams(vmem_limit_bytes=8 << 20),
        name="geometry",
    )(*sources)
    st_east, st_north = st_east.reshape(stations), st_north.reshape(stations)
    terms = lax.dot_general(
        probes,
        sensitivity(st_east, st_north, cell_geom),
        (((1,), (1,)), ((), ())),
        preferred_element_type=f32,
    )
    ends = [sum(FILLS[: i + 1]) for i in range(len(FILLS))]

    def kept(i, geometry):
        here = slice(ends[i] - FILLS[i], ends[i])
        st_east, st_north, *cell_geom = geometry
        return sensitivity(st_east[here], st_north[here], cell_geom)

    geometry = (st_east, st_north, *cell_geom)
    blocks = lax.axis_size(SCATTER)
    across = blocks // 2
    width = stations // across
    field = terms.reshape(2, 8, across, width).transpose(0, 2, 1, 3).reshape(blocks, 8, width)
    field, geometry = lax.optimization_barrier((field, geometry))
    parts, first = lax.optimization_barrier((exchanged(field, SCATTER), kept(0, geometry)))
    count = lax.axis_size(REDUCE)
    parts = called(copies_kernel, "reduced", jax.ShapeDtypeStruct((count, 8, width), f32), 1)(parts)
    parts, geometry = lax.optimization_barrier((parts, geometry))
    parts, second = lax.optimization_barrier((exchanged(parts, REDUCE), kept(1, geometry)))
    start = (lax.axis_index(SCATTER) % across) * width
    own_weight = lax.dynamic_slice_in_dim(station_weight, start, width).reshape(1, width)
    own = called(weigh_kernel, "weighed", jax.ShapeDtypeStruct((blocks, 8, width), jnp.bfloat16), 2)(parts, own_weight)
    own, geometry = lax.optimization_barrier((own, geometry))
    gathered, third = lax.optimization_barrier((exchanged(own, SCATTER), kept(2, geometry)))
    weighted = gathered.reshape(2, across, 8, width).transpose(0, 2, 1, 3).reshape(K, stations)
    backward = jnp.dot(
        weighted[:, ends[-1] :],
        sensitivity(geometry[0][ends[-1] :], geometry[1][ends[-1] :], geometry[2:]),
        preferred_element_type=f32,
    )
    for i, sens in enumerate((first, second, third)):
        segment = weighted[:, ends[i] - FILLS[i] : ends[i]]
        backward = backward + jnp.dot(segment, sens, preferred_element_type=f32)
    parts = exchanged(backward.reshape(K, cells // SPAN, SPAN).transpose(1, 0, 2), "yh")
    offset = lax.axis_index("yh") * SPAN
    own_reg = lax.dynamic_slice_in_dim(reg_weight, offset, SPAN).reshape(1, SPAN)
    own_probes = lax.dynamic_slice_in_dim(probes, offset, SPAN, 1)
    near, far = lax.axis_size(NEAR), lax.axis_size(FAR)
    image, grams = called(
        gram_kernel,
        "gram",
        (jax.ShapeDtypeStruct((K, SPAN), f32), jax.ShapeDtypeStruct((near, 2, 128), f32)),
        3,
    )(parts, own_reg, own_probes)
    grams = called(copies_kernel, "summed", jax.ShapeDtypeStruct((far, 2, 128), f32), 1)(exchanged(grams, NEAR))
    cell_total = float(cells * lax.axis_size(CELL_AXES))
    return called(
        functools.partial(solve_kernel, cell_total),
        "solve",
        (jax.ShapeDtypeStruct((K, SPAN), f32), jax.ShapeDtypeStruct((K, K), f32)),
        2,
    )(exchanged(grams, FAR), image)


def solution(mesh):
    split = Mesh(mesh.devices.reshape(8, 2, 4, 2, 4), ("z", "yl", "x", "c", "yh"))
    return jax.shard_map(
        body,
        mesh=split,
        in_specs=(
            P(None, CELL_AXES),
            P(CELL_AXES),
            P(None, CELL_AXES),
            P(CELL_AXES),
            P(None, "yh"),
            P("yh"),
        ),
        out_specs=(P(None, (*CELL_AXES, "yh")), P()),
        check_vma=False,
    )
```
